32 devices in a mesh: dp: 8 (over y, x, core), blk: 4 (over z).
Axes of the slice: x: 2, y: 2, z: 4, core: 2. Of those that a mesh axis runs over, the one named last changes fastest.
Arguments:
- tokens: bfloat16 [8, 2048, 1024], P('dp', 'blk'), may hold values from -6 to 6
- doc_starts: int32 [8, 3], P('dp'), may hold values from 0 to 2047, as said below
- qkv_weight: bfloat16 [1024, 3072], P(('dp', 'blk')), may hold values from -0.1875 to 0.1875
- out_weight: bfloat16 [1024, 1024], P(('dp', 'blk')), may hold values from -0.1875 to 0.1875
- up_weight: bfloat16 [1024, 4096], P(('dp', 'blk')), may hold values from -0.1875 to 0.1875
- down_weight: bfloat16 [4096, 1024], P(('dp', 'blk')), may hold values from -0.09375 to 0.09375
- norm_gains: bfloat16 [4, 1024], P(None, ('dp', 'blk')), may hold values from 0.25 to 1.75
- norm_biases: bfloat16 [4, 1024], P(None, ('dp', 'blk')), may hold values from -3 to 3
- cotangent: bfloat16 [8, 2048, 1024], P('dp', 'blk'), may hold values from -6 to 6
Outputs:
- layer_out: bfloat16 [8, 2048, 1024], P('dp', 'blk')
- grad_tokens: bfloat16 [8, 2048, 1024], P('dp', 'blk')
- grad_qkv: float32 [1024, 3072], P(('dp', 'blk'))
- grad_outproj: float32 [1024, 1024], P(('dp', 'blk'))
- grad_upproj: float32 [1024, 4096], P(('dp', 'blk'))
- grad_downproj: float32 [4096, 1024], P(('dp', 'blk'))
- grad_gains: float32 [4, 1024], P(None, ('dp', 'blk'))
- grad_biases: float32 [4, 1024], P(None, ('dp', 'blk'))
The draws below stay inside these ranges and needn't reach their ends.
Inputs may be any that keep to these rules, and one draw needn't show every extreme that they name: `doc_starts`: in each row the first start is 0 and the starts rise strictly; a document runs from its start to the next start or to the row's end. The first row's last document is its last place alone.
All inputs are finite; a program needn't handle non-finite values.
Results may differ from the reference program's by a relative error of at most 0.012.
Values may be sent and summed in bfloat16 or wider, within the bound.
No kernel may reach another device: no remote copies, remote signals or barrier semaphores. Data moves between devices by JAX's collectives and lax.ppermute only.
A program may use at most 256 MiB of HBM per device.

```python
import math
import jax
import jax.numpy as jnp
from jax import lax

D = 1024
HEADS = 16
HD = 64
FF = 4096
NDOC = 3
SEQ = 2048
ROWS = 8


def draw_doc_starts(key, part):
    row_keys = jax.random.split(key, ROWS)
    shuffled = jax.vmap(lambda row_key: jax.random.permutation(row_key, SEQ - 1))(row_keys)
    chosen = jnp.sort(shuffled[:, :NDOC - 1].astype(jnp.int32), axis=1) + 1
    chosen = chosen.at[0, NDOC - 2].set(SEQ - 1)
    return jnp.concatenate([jnp.zeros((ROWS, 1), jnp.int32), chosen], axis=1)


def block_levels(key, extent, shards, least, largest):
    gain, own = 1.0, jax.random.fold_in(key, 6)
    for axis_at, parts in shards:
        heights = jnp.exp(jax.random.uniform(jax.random.fold_in(own, axis_at), (parts,), jnp.float32, least / len(shards), largest / len(shards)))
        gain = gain * jnp.repeat(heights, extent[axis_at] // parts).reshape([-1 if axis == axis_at else 1 for axis in range(len(extent))])
    return gain


def centred(own_key, shape, spread, most, shards=(), kind=jnp.bfloat16):
    values = spread * jax.random.normal(own_key, shape, jnp.float32)
    if shards:
        values = values * block_levels(own_key, shape, shards, -0.22, 0.18)
    return jnp.clip(values, -most, most).astype(kind)


def setup_inputs(seed: int = 0) -> dict:
    key_of = jax.random.split(jax.random.key(seed), 10)
    tokens = centred(key_of[0], (ROWS, SEQ, D), 1.0, 6.0, ((0, 8), (1, 4)))
    doc_starts = draw_doc_starts(jax.random.fold_in(key_of[9], 71), 0)
    qkv_weight = centred(key_of[2], (D, 3 * D), D ** -0.5, 0.1875, ((0, 32),))
    out_weight = centred(key_of[3], (D, D), D ** -0.5, 0.1875, ((0, 32),))
    up_weight = centred(key_of[4], (D, FF), D ** -0.5, 0.1875, ((0, 32),))
    down_weight = centred(key_of[5], (FF, D), FF ** -0.5, 0.09375, ((0, 32),))
    norm_gains = jnp.clip(1.0 + 0.15 * jax.random.normal(key_of[6], (4, D), jnp.float32), 0.25, 1.75).astype(jnp.bfloat16)
    norm_biases = centred(key_of[7], (4, D), 0.5, 3.0, ((1, 32),))
    cotangent = centred(key_of[8], (ROWS, SEQ, D), 1.0, 6.0, ((0, 8), (1, 4)))
    return {"tokens": tokens, "doc_starts": doc_starts, "qkv_weight": qkv_weight, "out_weight": out_weight, "up_weight": up_weight, "down_weight": down_weight, "norm_gains": norm_gains, "norm_biases": norm_biases, "cotangent": cotangent}


@jax.custom_vjp
def low(v):
    return lax.optimization_barrier(v.astype(jnp.bfloat16)).astype(jnp.float32)

@jax.custom_vjp
def low_back(v):
    return v

def low_keep(v):
    return (low(v), None)

def low_pass(kept, grad):
    return (grad,)

def back_keep(v):
    return (v, None)

def back_low(kept, grad):
    return (low(grad),)
low.defvjp(low_keep, low_pass)
low_back.defvjp(back_keep, back_low)

def normalize(values, gain_row, bias_row):
    centered = values - lax.optimization_barrier(jnp.mean(values, axis=-1, keepdims=True))
    inverse = lax.rsqrt(lax.optimization_barrier(jnp.mean(centered * centered, axis=-1, keepdims=True)) + 1e-05)
    return centered * inverse * gain_row + bias_row

def document_layout(starts, first, count):
    places = first + jnp.arange(count, dtype=jnp.int32)
    inside = starts[None, :] <= places[:, None]
    segment = lax.optimization_barrier(jnp.sum(inside.astype(jnp.int32), axis=1))
    opening = lax.optimization_barrier(jnp.max(jnp.where(inside, starts[None, :], 0), axis=1))
    return (places, segment, places - opening)

def rotary_tables(positions, head_size):
    halfway = head_size // 2
    frequency = jnp.exp(jnp.arange(halfway, dtype=jnp.float32) * (-2.0 * math.log(10000.0) / head_size))
    angles = positions.astype(jnp.float32)[:, None] * frequency[None, :]
    cosine = jnp.concatenate([jnp.cos(angles), jnp.cos(angles)], axis=-1)[:, None, :]
    sine_part = jnp.concatenate([jnp.sin(angles), jnp.sin(angles)], axis=-1)[:, None, :]
    return (cosine, sine_part)

def rotate(values, cosine, sine_part):
    halfway = values.shape[-1] // 2
    turned = jnp.concatenate([-values[..., halfway:], values[..., :halfway]], axis=-1)
    return values * cosine + turned * sine_part

def attend(queries, keys, values, segment, places):
    block_rows = min(512, SEQ)
    count = SEQ // block_rows
    query_blocks = queries.reshape(count, block_rows, HEADS, HD)
    firsts = jnp.arange(count, dtype=jnp.int32) * block_rows
    factor = HD ** (-0.5)

    def one_block(pieces):
        query_part, first = pieces
        query_places = first + jnp.arange(block_rows, dtype=jnp.int32)
        query_segment = lax.dynamic_slice_in_dim(segment, first, block_rows)
        scores = low_back(jnp.einsum('qhd,khd->hqk', query_part, keys, precision=lax.Precision.HIGHEST) * factor)
        allowed = (query_segment[:, None] == segment[None, :]) & (places[None, :] <= query_places[:, None])
        scores = jnp.where(allowed[None], scores, -1e+30)
        highest = lax.optimization_barrier(jnp.max(scores, axis=-1, keepdims=True))
        expsum = jnp.exp(scores - highest)
        probs = low(expsum / lax.optimization_barrier(jnp.sum(expsum, axis=-1, keepdims=True)))
        return jnp.einsum('hqk,khd->qhd', probs, values, precision=lax.Precision.HIGHEST)
    result = lax.map(jax.checkpoint(one_block), (query_blocks, firsts))
    return result.reshape(SEQ, HEADS * HD)

def reference(tokens, doc_starts, qkv_weight, out_weight, up_weight, down_weight, norm_gains, norm_biases, cotangent):
    weights = (qkv_weight.astype(jnp.float32), out_weight.astype(jnp.float32), up_weight.astype(jnp.float32), down_weight.astype(jnp.float32), norm_gains.astype(jnp.float32), norm_biases.astype(jnp.float32))

    def one_row(running, row_data):
        row_tokens, starts, row_cot = row_data
        places, segment, positions = document_layout(starts, 0, SEQ)
        cosine, sine_part = rotary_tables(positions, HD)

        def forward(inputs, full_qkv, full_out, full_up, full_down, gains, biases):
            normed = normalize(inputs, gains[0], biases[0])
            projected = low_back(jnp.dot(low(normed), full_qkv, precision=lax.Precision.HIGHEST))
            queries = low(rotate(projected[:, :D].reshape(SEQ, HEADS, HD), cosine, sine_part))
            keys = low(rotate(projected[:, D:2 * D].reshape(SEQ, HEADS, HD), cosine, sine_part))
            values = low(projected[:, 2 * D:].reshape(SEQ, HEADS, HD))
            attended = low(low_back(attend(queries, keys, values, segment, places)))
            output_proj = low_back(jnp.dot(attended, full_out, precision=lax.Precision.HIGHEST))
            hidden = inputs + normalize(output_proj, gains[1], biases[1])
            second = low(normalize(hidden, gains[2], biases[2]))
            expanded = low_back(jnp.dot(second, full_up, precision=lax.Precision.HIGHEST))
            shrunk = low_back(jnp.dot(low(jax.nn.gelu(expanded, approximate=True)), full_down, precision=lax.Precision.HIGHEST))
            return hidden + normalize(shrunk, gains[3], biases[3])
        result, pullback = jax.vjp(forward, row_tokens.astype(jnp.float32), *weights)
        grads = pullback(row_cot.astype(jnp.float32))
        running = tuple((total + piece for total, piece in zip(running, grads[1:])))
        return (running, (result.astype(jnp.bfloat16), grads[0].astype(jnp.bfloat16)))
    initial = tuple((jnp.zeros_like(weight) for weight in weights))
    totals, (outputs, input_grads) = lax.scan(one_row, initial, (tokens, doc_starts, cotangent))
    return (outputs, input_grads, totals[0], totals[1], totals[2], totals[3], totals[4], totals[5])
```

```python
import functools
import math

import jax
import jax.numpy as jnp
from jax import lax
from jax.experimental import pallas as pl
from jax.experimental.pallas import tpu as pltpu
from jax.sharding import Mesh, PartitionSpec as P

HEADS = 16
HD = 64
NEG = -1e30
BF = jnp.bfloat16
F32 = jnp.float32
NT = (((1,), (1,)), ((), ()))
VMEM = 60 * 1024 * 1024


def normalize(values, gain_row, bias_row):
    centered = values - jnp.mean(values, axis=-1, keepdims=True)
    inverse = lax.rsqrt(jnp.mean(centered * centered, axis=-1, keepdims=True) + 1e-05)
    unit_rows = centered * inverse
    return (unit_rows * gain_row + bias_row, unit_rows, inverse)


def normalize_back(upstream, unit_rows, inverse, gain_row):
    scaled = upstream * gain_row
    bracket = (
        scaled
        - jnp.mean(scaled, axis=-1, keepdims=True)
        - unit_rows * jnp.mean(scaled * unit_rows, axis=-1, keepdims=True)
    )
    return (inverse * bracket, jnp.sum(upstream * unit_rows, axis=0), jnp.sum(upstream, axis=0))


def turn(values, first_half):
    return jnp.where(
        first_half, pltpu.roll(values, 96, axis=1), pltpu.roll(values, 32, axis=1)
    )


def opening(starts_ref, count, place):
    opened = jnp.int32(0)
    for d in range(count):
        s = starts_ref[0, d]
        opened = jnp.where(s <= place, jnp.maximum(opened, s), opened)
    return opened


def closing(starts_ref, count, place, length):
    closed = jnp.int32(length)
    for d in range(count):
        s = starts_ref[0, d]
        closed = jnp.where(s > place, jnp.minimum(closed, s), closed)
    return closed


def qkv_kernel(a_ref, w_ref, cos_ref, sin_ref, q_ref, k_ref, v_ref, kt_ref, vt_ref):
    width = q_ref.shape[1]
    prod = jnp.dot(a_ref[...], w_ref[...], preferred_element_type=F32)
    rows = prod.shape[0]
    first_half = lax.broadcasted_iota(jnp.int32, (rows, 128), 1) % HD < HD // 2
    cosine, sine = cos_ref[...], sin_ref[...]
    for s in range(width // 128):
        lanes = slice(128 * s, 128 * (s + 1))
        e = prod[:, lanes]
        q_ref[:, lanes] = ((e * cosine + turn(e, first_half) * sine) * HD**-0.5).astype(BF)
        e = prod[:, width + 128 * s : width + 128 * (s + 1)]
        k = (e * cosine + turn(e, first_half) * sine).astype(BF)
        k_ref[:, lanes] = k
        kt_ref[lanes, :] = k.T
        v = prod[:, 2 * width + 128 * s : 2 * width + 128 * (s + 1)].astype(BF)
        v_ref[:, lanes] = v
        vt_ref[lanes, :] = v.T


def qkv_call(a_all, w, cosine, sine, rows):
    length, depth = a_all.shape
    width = w.shape[1] // 3
    flat = jax.ShapeDtypeStruct((length, width), BF)
    turned = jax.ShapeDtypeStruct((width, length), BF)
    return pl.pallas_call(
        qkv_kernel,
        grid=(length // rows,),
        in_specs=[
            pl.BlockSpec((rows, depth), lambda i: (i, 0)),
            pl.BlockSpec((depth, 3 * width), lambda i: (0, 0)),
            pl.BlockSpec((rows, 128), lambda i: (i, 0)),
            pl.BlockSpec((rows, 128), lambda i: (i, 0)),
        ],
        out_specs=[pl.BlockSpec((rows, width), lambda i: (i, 0))] * 3
        + [pl.BlockSpec((width, rows), lambda i: (0, i))] * 2,
        out_shape=[flat, flat, flat, turned, turned],
        compiler_params=pltpu.CompilerParams(vmem_limit_bytes=VMEM),
        cost_estimate=pl.CostEstimate(
            flops=6 * length * depth * width,
            bytes_accessed=2 * length * depth + 10 * length * width,
            transcendentals=0,
        ),
        name="qkv_rope",
    )(a_all, w, cosine, sine)


def allowed_bias(starts_ref, count, kfirst, qfirst, bk, bq):
    kpos = kfirst + lax.broadcasted_iota(jnp.int32, (bk, bq), 0)
    qrow = qfirst + lax.broadcasted_iota(jnp.int32, (1, bq), 1)
    opened = jnp.zeros((1, bq), jnp.int32)
    for d in range(count):
        s = starts_ref[0, d]
        opened = jnp.where(s <= qrow, jnp.maximum(opened, s), opened)
    return jnp.where((kpos >= opened) & (kpos <= qrow), 0.0, NEG)


def head_lanes(rows, which):
    return lax.broadcasted_iota(jnp.int32, (rows, 128), 1) // HD == which


def forward_kernel(starts_ref, q_ref, k_ref, vt_ref, att_ref, lse_ref, *, bk):
    count = starts_ref.shape[1]
    bq, width = q_ref.shape
    heads = width // HD
    i = pl.program_id(0)
    first = i * bq
    low = opening(starts_ref, count, first) // bk
    high = (first + bq - 1) // bk + 1
    masked = []
    for h in range(heads):
        pair = q_ref[:, 128 * (h // 2) : 128 * (h // 2 + 1)]
        masked.append(jnp.where(head_lanes(bq, h % 2), pair, jnp.zeros_like(pair)))

    def step(j, carry):
        bias = allowed_bias(starts_ref, count, j * bk, first, bk, bq)
        at = pl.ds(pl.multiple_of(j * bk, bk), bk)
        new = []
        for h in range(heads):
            peak, total, acc = carry[h]
            keys = k_ref[at, 128 * (h // 2) : 128 * (h // 2 + 1)]
            scores = lax.dot_general(keys, masked[h], NT, preferred_element_type=F32) + bias
            higher = jnp.maximum(peak, jnp.max(scores, axis=0, keepdims=True))
            probs = jnp.exp(scores - higher)
            shrink = jnp.exp(peak - higher)
            total = total * shrink + jnp.sum(probs, axis=0, keepdims=True)
            acc = acc * shrink + jnp.dot(
                vt_ref[HD * h : HD * (h + 1), at], probs.astype(BF), preferred_element_type=F32
            )
            new.append((higher, total, acc))
        return tuple(new)

    begin = tuple(
        (jnp.full((1, bq), NEG, F32), jnp.zeros((1, bq), F32), jnp.zeros((HD, bq), F32))
        for _ in range(heads)
    )
    done = lax.fori_loop(low, high, step, begin)
    for h in range(heads):
        peak, total, acc = done[h]
        lse_ref[h : h + 1, :] = peak + jnp.log(total)
    att = jnp.concatenate([acc / total for _, total, acc in done], axis=0)
    att_ref[...] = att.astype(BF).T


def forward_call(starts, q, k, vt, bq, bk):
    length, width = q.shape
    heads = width // HD
    return pl.pallas_call(
        functools.partial(forward_kernel, bk=bk),
        grid_spec=pltpu.PrefetchScalarGridSpec(
            num_scalar_prefetch=1,
            grid=(length // bq,),
            in_specs=[
                pl.BlockSpec((bq, width), lambda i, s: (i, 0)),
                pl.BlockSpec((length, width), lambda i, s: (0, 0)),
                pl.BlockSpec((width, length), lambda i, s: (0, 0)),
            ],
            out_specs=[
                pl.BlockSpec((bq, width), lambda i, s: (i, 0)),
                pl.BlockSpec((heads, bq), lambda i, s: (0, i)),
            ],
        ),
        out_shape=[
            jax.ShapeDtypeStruct((length, width), BF),
            jax.ShapeDtypeStruct((heads, length), F32),
        ],
        compiler_params=pltpu.CompilerParams(vmem_limit_bytes=VMEM),
        cost_estimate=pl.CostEstimate(
            flops=8 * length * length * width,
            bytes_accessed=8 * length * width,
            transcendentals=length * length * heads // 2,
        ),
        name="attend",
    )(starts, q, k, vt)


def backward_kernel(
    starts_ref, q_ref, g_ref, k_ref, v_ref, kt_ref, lse_ref, dot_ref, cos_ref, sin_ref, out_ref, dqt_ref, *, bq
):
    count = starts_ref.shape[1]
    length, width = q_ref.shape
    bk = k_ref.shape[0]
    heads = width // HD
    j = pl.program_id(0)
    kfirst = j * bk

    @pl.when(j == 0)
    def _():
        dqt_ref[...] = jnp.zeros_like(dqt_ref)

    low = kfirst // bq
    high = (closing(starts_ref, count, kfirst + bk - 1, length) - 1) // bq + 1

    def step(i, carry):
        bias = allowed_bias(starts_ref, count, kfirst, i * bq, bk, bq)
        at = pl.ds(pl.multiple_of(i * bq, bq), bq)
        dks, dvs = list(carry[0]), list(carry[1])
        for h in range(heads):
            s = h // 2
            lanes = slice(128 * s, 128 * (s + 1))
            mine = head_lanes(bq, h % 2)
            queries = q_ref[at, lanes]
            queries = jnp.where(mine, queries, jnp.zeros_like(queries))
            grads = g_ref[at, lanes]
            grads = jnp.where(mine, grads, jnp.zeros_like(grads))
            scores = lax.dot_general(k_ref[:, lanes], queries, NT, preferred_element_type=F32)
            probs = jnp.exp(scores + (bias - lse_ref[h : h + 1, at]))
            dprobs = lax.dot_general(v_ref[:, lanes], grads, NT, preferred_element_type=F32)
            dscores = (probs * (dprobs - dot_ref[h : h + 1, at])).astype(BF)
            dvs[s] = dvs[s] + jnp.dot(probs.astype(BF), grads, preferred_element_type=F32)
            dks[s] = dks[s] + jnp.dot(dscores, queries, preferred_element_type=F32)
            rows = slice(HD * h, HD * (h + 1))
            dqt_ref[rows, at] += jnp.dot(kt_ref[rows, :], dscores, preferred_element_type=F32)
        return (tuple(dks), tuple(dvs))

    zeros = tuple(jnp.zeros((bk, 128), F32) for _ in range(width // 128))
    dks, dvs = lax.fori_loop(low, high, step, (zeros, zeros))
    here = pl.ds(pl.multiple_of(kfirst, bk), bk)

    def back(values, at, rows):
        first_half = lax.broadcasted_iota(jnp.int32, (rows, 128), 1) % HD < HD // 2
        return values * cos_ref[at, :] - turn(values, first_half) * sin_ref[at, :]

    for s in range(width // 128):
        low_lane = width + 128 * s
        out_ref[here, low_lane : low_lane + 128] = back(dks[s], here, bk).astype(BF)
        out_ref[here, width + low_lane : width + low_lane + 128] = dvs[s].astype(BF)

    @pl.when(j == pl.num_programs(0) - 1)
    def _():
        for b in range(length // bq):
            at = slice(b * bq, (b + 1) * bq)
            dq = dqt_ref[:, at].T * HD**-0.5
            for s in range(width // 128):
                lanes = slice(128 * s, 128 * (s + 1))
                out_ref[at, lanes] = back(dq[:, lanes], at, bq).astype(BF)


def backward_call(starts, q, g, k, v, kt, lse, dots, cosine, sine, bq, bk):
    length, width = q.shape
    heads = width // HD
    whole = lambda j, s: (0, 0)
    return pl.pallas_call(
        functools.partial(backward_kernel, bq=bq),
        grid_spec=pltpu.PrefetchScalarGridSpec(
            num_scalar_prefetch=1,
            grid=(length // bk,),
            in_specs=[
                pl.BlockSpec((length, width), whole),
                pl.BlockSpec((length, width), whole),
                pl.BlockSpec((bk, width), lambda j, s: (j, 0)),
                pl.BlockSpec((bk, width), lambda j, s: (j, 0)),
                pl.BlockSpec((width, bk), lambda j, s: (0, j)),
                pl.BlockSpec((heads, length), whole),
                pl.BlockSpec((heads, length), whole),
                pl.BlockSpec((length, 128), whole),
                pl.BlockSpec((length, 128), whole),
            ],
            out_specs=pl.BlockSpec((length, 3 * width), whole),
            scratch_shapes=[pltpu.VMEM((width, length), F32)],
        ),
        out_shape=jax.ShapeDtypeStruct((length, 3 * width), BF),
        compiler_params=pltpu.CompilerParams(vmem_limit_bytes=VMEM),
        cost_estimate=pl.CostEstimate(
            flops=20 * length * length * width,
            bytes_accessed=20 * length * width,
            transcendentals=length * length * heads // 2,
        ),
        name="attend_back",
    )(starts, q, g, k, v, kt, lse, dots, cosine, sine)


def build(cubes):
    axes = cubes + ("core", "zh", "zl")
    rank = len(axes)
    ring = ("core", "zh", "zl")

    def swap(x, ax):
        return lax.ppermute(x, ax, [(0, 1), (1, 0)])

    def grow(x, ax):
        d, i = axes.index(ax), lax.axis_index(ax)
        other = swap(x, ax)
        return lax.dynamic_update_slice_in_dim(jnp.concatenate([x, x], d), other, 1 - i, d)

    def gather(x, order):
        for ax in order:
            x = grow(x, ax)
        return x

    def lone(x):
        return x.reshape((1,) * rank + x.shape)

    def spread(g, rows):
        sizes = (2,) * rank
        return g.reshape(sizes + (rows,) + g.shape[1:])

    def halve(g, ax, kept, sent=BF):
        d, i = axes.index(ax), lax.axis_index(ax)
        keep = lax.dynamic_slice_in_dim(g, i, 1, d)
        send = lax.dynamic_slice_in_dim(g, 1 - i, 1, d)
        got = swap(send.astype(sent), ax)
        return (keep.astype(F32) + got.astype(F32)).astype(kept)

    def reduce(g, order, sent=BF):
        for n, ax in enumerate(order):
            g = halve(g, ax, F32 if n == len(order) - 1 else sent, sent)
        return g

    def exchange(x, ax, d):
        i = lax.axis_index(ax)
        got = swap(lax.dynamic_slice_in_dim(x, 1 - i, 1, d), ax)
        return lax.dynamic_update_slice_in_dim(x, got, 1 - i, d)

    there = [
        (c * 4 + zh * 2 + zl, zl * 4 + c * 2 + zh)
        for c in range(2) for zh in range(2) for zl in range(2)
    ]
    home = [(b, a) for a, b in there]

    def move(x, table):
        return lax.ppermute(x, ring, table)

    def per_device(tokens, doc_starts, qkv_w, out_w, up_w, down_w, norm_gains, norm_biases, cotangent):
        length, depth = tokens.shape[1:]
        full = 4 * length
        width = depth // 4
        ff = up_w.shape[1]
        norm_rows = norm_gains.shape[0]

        inputs_low = move(tokens[0], there)
        starts = move(doc_starts, there)
        params = jnp.concatenate([norm_gains, norm_biases], 0)
        params = gather(lone(params), axes[::-1])
        params = params.reshape((-1,) + params.shape[rank:]).transpose(1, 0, 2)
        params = params.reshape(2 * norm_rows, depth).astype(F32)
        gains, biases = params[:norm_rows], params[norm_rows:]

        w = qkv_w.reshape(-1, 3, 2, 2, width).transpose(2, 3, 0, 1, 4)
        w = w.reshape(2, 2, qkv_w.shape[0], 3 * width)
        w = exchange(exchange(w, "zl", 0), "core", 1)
        w = w.transpose(1, 0, 2, 3)
        w = w.reshape((1,) * len(cubes) + (2, 1, 2) + w.shape[2:])
        full_qkv = gather(w, ("zh",) + cubes[::-1]).reshape(depth, 3 * width)
        full_out = gather(lone(out_w), ("zl", "zh") + cubes + ("core",)).reshape(depth, depth)
        full_up = gather(lone(up_w), ("zl", "zh") + cubes[::-1] + ("core",)).reshape(depth, ff)
        full_down = gather(lone(down_w), ("zl", "zh") + cubes + ("core",)).reshape(ff, depth)
        upstream_low = move(cotangent[0], there)

        places = jnp.arange(full, dtype=jnp.int32)
        inside = starts[0][None, :] <= places[:, None]
        opened = jnp.max(jnp.where(inside, starts[0][None, :], 0), axis=1)
        positions = (places - opened).astype(F32)
        half = HD // 2
        frequency = jnp.exp(jnp.arange(half, dtype=F32) * (-2.0 * math.log(10000.0) / HD))
        angles = positions[:, None] * frequency[None, :]
        cosine, sine = jnp.cos(angles), jnp.sin(angles)
        cosine = jnp.concatenate([cosine] * 4, axis=1)
        sine = jnp.concatenate([-sine, sine] * 2, axis=1)

        inputs = inputs_low.astype(F32)
        normed, first_unit, first_inverse = normalize(inputs, gains[0], biases[0])
        first_low = normed.astype(BF)
        group = first_low.reshape((1, 1) + first_low.shape)

        def widen(x, ax, d):
            i = lax.axis_index(ax)
            other = swap(x, ax)
            return lax.dynamic_update_slice_in_dim(jnp.concatenate([x, x], d), other, 1 - i, d)

        a_all = widen(widen(group, "zl", 0), "core", 1).reshape(full, depth)
        q, k, v, kt, vt = qkv_call(a_all, full_qkv, cosine, sine, min(512, full))
        att, lse = forward_call(starts, q, k, vt, 256, 256)
        parts = att.reshape(2, 2, length, width)
        parts = exchange(exchange(parts, "zl", 0), "core", 1)
        att_low = parts.transpose(2, 0, 1, 3).reshape(length, depth)
        output_proj = jnp.dot(att_low, full_out, preferred_element_type=F32)
        normed_out, out_unit, out_inverse = normalize(output_proj, gains[1], biases[1])
        hidden = inputs + normed_out
        second, second_unit, second_inverse = normalize(hidden, gains[2], biases[2])
        second_low = second.astype(BF)
        expanded = jnp.dot(second_low, full_up, preferred_element_type=F32)
        activated, gelu_pull = jax.vjp(lambda values: jax.nn.gelu(values, approximate=True), expanded)
        activated_low = activated.astype(BF)
        shrunk = jnp.dot(activated_low, full_down, preferred_element_type=F32)
        normed_last, last_unit, last_inverse = normalize(shrunk, gains[3], biases[3])
        layer_out = move((hidden + normed_last).astype(BF), home)

        upstream = upstream_low.astype(F32)
        d_shrunk, grad_gain3, grad_bias3 = normalize_back(upstream, last_unit, last_inverse, gains[3])
        d_shrunk_low = d_shrunk.astype(BF)
        grad_down = jnp.einsum("tf,td->fd", activated_low, d_shrunk_low, preferred_element_type=F32)
        d_activated = jnp.einsum("td,fd->tf", d_shrunk_low, full_down, preferred_element_type=F32)
        d_expanded_low = gelu_pull(d_activated)[0].astype(BF)
        grad_up = jnp.einsum("tc,tf->cf", second_low, d_expanded_low, preferred_element_type=F32)
        d_second = jnp.einsum("tf,cf->tc", d_expanded_low, full_up, preferred_element_type=F32)
        d_from_second, grad_gain2, grad_bias2 = normalize_back(
            d_second, second_unit, second_inverse, gains[2]
        )
        d_hidden = upstream + d_from_second
        d_output, grad_gain1, grad_bias1 = normalize_back(d_hidden, out_unit, out_inverse, gains[1])
        d_output_low = d_output.astype(BF)
        grad_out = jnp.einsum("tc,td->cd", att_low, d_output_low, preferred_element_type=F32)
        d_att = jnp.einsum("td,cd->tc", d_output_low, full_out, preferred_element_type=F32).astype(BF)
        parts = d_att.reshape(length, 2, 2, width).transpose(1, 2, 0, 3)
        parts = exchange(exchange(parts, "zl", 0), "core", 1)
        d_heads = parts.reshape(full, width)
        dots = (d_heads.astype(F32) * att.astype(F32)).reshape(full, width // HD, HD).sum(-1).T
        d_qkv = backward_call(starts, q, d_heads, k, v, kt, lse, dots, cosine, sine, 256, 256)
        grad_qkv = jnp.einsum("tc,tk->ck", a_all, d_qkv, preferred_element_type=F32)
        d_first = jnp.einsum("tk,ck->tc", d_qkv, full_qkv, preferred_element_type=F32).astype(BF)
        d_first = d_first.reshape(2, 2, length, depth)

        def fold(x, ax, d):
            i = lax.axis_index(ax)
            got = swap(lax.dynamic_slice_in_dim(x, 1 - i, 1, d).astype(BF), ax)
            return lax.dynamic_slice_in_dim(x, i, 1, d).astype(F32) + got.astype(F32)

        d_first = fold(fold(d_first, "core", 1), "zl", 0).reshape(length, depth)
        d_from_first, grad_gain0, grad_bias0 = normalize_back(
            d_first, first_unit, first_inverse, gains[0]
        )
        grad_inputs = move((d_hidden + d_from_first).astype(BF), home)

        sum_up = reduce(spread(grad_up.astype(BF), up_w.shape[0]), ("core",) + cubes + ("zh", "zl"))
        sum_down = reduce(
            spread(grad_down.astype(BF), down_w.shape[0]), ("core",) + cubes[::-1] + ("zh", "zl")
        )
        sum_out = reduce(
            spread(grad_out.astype(BF), out_w.shape[0]), ("core",) + cubes[::-1] + ("zh", "zl")
        )
        g = reduce(spread(grad_qkv.astype(BF), qkv_w.shape[0]), cubes + ("zh",))
        g = g.reshape((2, 2) + g.shape[rank:])
        g = exchange(exchange(g, "core", 0), "zl", 1)
        g = g.reshape(2, 2, -1, 3, width).transpose(2, 3, 1, 0, 4)
        sum_qkv = g.reshape(qkv_w.shape)
        rows = jnp.stack(
            [grad_gain0, grad_gain1, grad_gain2, grad_gain3, grad_bias0, grad_bias1, grad_bias2, grad_bias3]
        )
        rows = rows.reshape(2 * norm_rows, 2**rank, -1).transpose(1, 0, 2)
        rows = rows.reshape((2,) * rank + rows.shape[1:])
        rows = reduce(rows, axes, F32).reshape(2 * norm_rows, -1)
        return (
            layer_out[None],
            grad_inputs[None],
            sum_qkv,
            sum_out.reshape(out_w.shape),
            sum_up.reshape(up_w.shape),
            sum_down.reshape(down_w.shape),
            rows[:norm_rows],
            rows[norm_rows:],
        )

    return per_device


def solution(mesh):
    dp, blk = mesh.shape["dp"], mesh.shape["blk"]
    assert blk == 4 and dp & (dp - 1) == 0
    cubes = tuple(f"h{i}" for i in range(dp.bit_length() - 2))
    axes = cubes + ("core", "zh", "zl")
    devices = mesh.devices.reshape((2,) * len(axes))
    fine = Mesh(devices, axes)
    rows, blocks = cubes + ("core",), ("zh", "zl")
    tokens = P(rows, blocks, None)
    first, second = P(axes, None), P(None, axes)
    return jax.shard_map(
        build(cubes),
        mesh=fine,
        in_specs=(tokens, P(rows, None), first, first, first, first, second, second, tokens),
        out_specs=(tokens, tokens, first, first, first, first, second, second),
        check_vma=False,
    )
```
